512 devices in a mesh: leaf: 64 (over y, x, core), panel: 8 (over z).
Axes of the slice: x: 4, y: 8, z: 8, core: 2. Of those that a mesh axis runs over, the one named last changes fastest.
Arguments:
- rhs_0: bfloat16 [4096, 1024], P('leaf', 'panel'), may hold values from -6 to 6
- rhs_1: bfloat16 [4096, 1024], P('leaf', 'panel'), may hold values from -6 to 6
- rhs_2: bfloat16 [4096, 1024], P('leaf', 'panel'), may hold values from -6 to 6
- rhs_3: bfloat16 [4096, 1024], P('leaf', 'panel'), may hold values from -6 to 6
- inv_0: bfloat16 [4096, 4096], P(('leaf', 'panel')), as said below
- inv_1: bfloat16 [4096, 2048], P(('leaf', 'panel')), as said below
- inv_2: bfloat16 [4096, 1024], P(('leaf', 'panel')), as said below
- inv_3: bfloat16 [4096, 512], P(('leaf', 'panel')), as said below
- coupling_1: bfloat16 [4096, 2048], P(('leaf', 'panel')), may hold values from -0.125 to 0.125
- coupling_2: bfloat16 [4096, 1024], P(('leaf', 'panel')), may hold values from -0.1875 to 0.1875
- coupling_3: bfloat16 [4096, 512], P(('leaf', 'panel')), may hold values from -0.25 to 0.25
- update_rows_1: int32 [2, 2048], replicated, may hold values from 0 to 4095, as said below
- update_rows_2: int32 [4, 1024], replicated, may hold values from 0 to 6143, as said below
- update_rows_3: int32 [8, 512], replicated, may hold values from 0 to 7167, as said below
Outputs:
- solution_0: bfloat16 [4096, 1024], P('leaf', 'panel')
- solution_1: bfloat16 [4096, 1024], P('leaf', 'panel')
- solution_2: bfloat16 [4096, 1024], P('leaf', 'panel')
- solution_3: bfloat16 [4096, 1024], P('leaf', 'panel')
The draws below stay inside these ranges and needn't reach their ends.
Inputs may be any that keep to these rules, and one draw needn't show every extreme that they name: `update_rows_1`: row f lists the update rows of front f of depth 1: 2048 distinct indices into its ancestor rows, holding 0 and the last ancestor row. `update_rows_2`: row f lists the update rows of front f of depth 2: 1024 distinct indices into its ancestor rows, holding 0 and the last ancestor row. `update_rows_3`: row f lists the update rows of front f of depth 3: 512 distinct indices into its ancestor rows, holding 0 and the last ancestor row. `inv_0`: the block is lower triangular with its diagonal between 0.5 and 2. `inv_1`: each 2048-row block is lower triangular with its diagonal between 0.5 and 2. `inv_2`: each 1024-row block is lower triangular with its diagonal between 0.5 and 2. `inv_3`: each 512-row block is lower triangular with its diagonal between 0.5 and 2.
All inputs are finite; a program needn't handle non-finite values.
Results may differ from the reference program's by a relative error of at most 0.014.
Values may be sent and summed in bfloat16 or wider, within the bound.
No kernel may reach another device: no remote copies, remote signals or barrier semaphores. Data moves between devices by JAX's collectives and lax.ppermute only.
A program may use at most 64 MiB of HBM per device.

```python
import math
import jax
import jax.numpy as jnp

PIVOTS = 4096
LEVELS = 4
RHS = 1024


def lower_inverse(key, front_rows):
    noise_draw = jax.random.normal(key, (PIVOTS, front_rows), jnp.float32)
    row_within = jnp.arange(PIVOTS, dtype=jnp.int32) % front_rows
    column_ids = jnp.arange(front_rows, dtype=jnp.int32)
    below = column_ids[None, :] < row_within[:, None]
    on_diagonal = column_ids[None, :] == row_within[:, None]
    diag_key = jax.random.fold_in(key, 7)
    diag_values = jnp.exp(jax.random.uniform(diag_key, (PIVOTS,), jnp.float32, math.log(0.5), math.log(2.0)))
    spread = 0.7
    lower_part = jnp.where(below, noise_draw * (spread / math.sqrt(front_rows)), 0.0)
    values = lower_part + jnp.where(on_diagonal, diag_values[:, None], 0.0)
    return values.astype(jnp.bfloat16)


def draw_inv_0(key, part):
    return lower_inverse(key, PIVOTS)


def draw_inv_1(key, part):
    return lower_inverse(key, PIVOTS // 2)


def draw_inv_2(key, part):
    return lower_inverse(key, PIVOTS // 4)


def draw_inv_3(key, part):
    return lower_inverse(key, PIVOTS // 8)


def ancestor_lists(key, depth_now):
    list_length = PIVOTS >> depth_now
    span_rows = 0
    for upper in range(depth_now):
        span_rows = span_rows + (PIVOTS >> upper)
    row_lists = []
    for front in range(2 ** depth_now):
        node_key = jax.random.fold_in(key, 100 * depth_now + front)
        inner = jax.random.permutation(node_key, span_rows - 2)[:list_length - 2].astype(jnp.int32) + 1
        joined = jnp.concatenate([jnp.zeros((1,), jnp.int32), inner, jnp.full((1,), span_rows - 1, jnp.int32)])
        order_key = jax.random.fold_in(node_key, 11)
        shuffled = jax.random.permutation(order_key, list_length)
        row_lists.append(joined[shuffled])
    return jnp.stack(row_lists).astype(jnp.int32)


def draw_update_rows_1(key, part):
    return ancestor_lists(key, 1)


def draw_update_rows_2(key, part):
    return ancestor_lists(key, 2)


def draw_update_rows_3(key, part):
    return ancestor_lists(key, 3)


def block_scale(stream_key, dims, cuts, smallest, largest):
    def one(position, parts):
        steps = jax.random.uniform(jax.random.fold_in(jax.random.fold_in(stream_key, 6), position), (parts,), jnp.float32, smallest / len(cuts), largest / len(cuts))
        return jnp.repeat(jnp.exp(steps), dims[position] // parts).reshape((-1,) + (1,) * (len(dims) - position - 1))

    factor_of = one(*cuts[0])
    for cut in cuts[1:]:
        factor_of = factor_of * one(*cut)
    return factor_of


def bell_draw(rng, extent, deviation, most, cuts=(), kind=jnp.bfloat16):
    level = block_scale(rng, extent, cuts, -0.22, 0.18) if cuts else 1.0
    values = jax.random.normal(rng, extent, jnp.float32) * deviation * level
    return jnp.minimum(jnp.maximum(values, -most), most).astype(kind)


def setup_inputs(seed: int = 0) -> dict:
    keys = jax.random.split(jax.random.key(seed), 15)
    return {
        "rhs_0": bell_draw(keys[0], (PIVOTS, RHS), 1.0, 6.0, ((0, 64), (1, 8))),
        "rhs_1": bell_draw(keys[1], (PIVOTS, RHS), 1.0, 6.0, ((0, 64), (1, 8))),
        "rhs_2": bell_draw(keys[2], (PIVOTS, RHS), 1.0, 6.0, ((0, 64), (1, 8))),
        "rhs_3": bell_draw(keys[3], (PIVOTS, RHS), 1.0, 6.0, ((0, 64), (1, 8))),
        "inv_0": draw_inv_0(jax.random.fold_in(keys[14], 71), 0),
        "inv_1": draw_inv_1(jax.random.fold_in(keys[14], 71), 0),
        "inv_2": draw_inv_2(jax.random.fold_in(keys[14], 71), 0),
        "inv_3": draw_inv_3(jax.random.fold_in(keys[14], 71), 0),
        "coupling_1": bell_draw(keys[8], (PIVOTS, PIVOTS // 2), (PIVOTS // 2) ** -0.5, 0.125, ((0, 512),)),
        "coupling_2": bell_draw(keys[9], (PIVOTS, PIVOTS // 4), (PIVOTS // 4) ** -0.5, 0.1875, ((0, 512),)),
        "coupling_3": bell_draw(keys[10], (PIVOTS, PIVOTS // 8), (PIVOTS // 8) ** -0.5, 0.25, ((0, 512),)),
        "update_rows_1": draw_update_rows_1(jax.random.fold_in(keys[14], 71), 0),
        "update_rows_2": draw_update_rows_2(jax.random.fold_in(keys[14], 71), 0),
        "update_rows_3": draw_update_rows_3(jax.random.fold_in(keys[14], 71), 0),
    }


def reference(rhs_0, rhs_1, rhs_2, rhs_3, inv_0, inv_1, inv_2, inv_3, coupling_1, coupling_2, coupling_3, update_rows_1, update_rows_2, update_rows_3):
    rhs_all = [rhs_0, rhs_1, rhs_2, rhs_3]
    inv_all = [inv_0, inv_1, inv_2, inv_3]
    coupling_all = [None, coupling_1, coupling_2, coupling_3]
    lists_all = [None, update_rows_1, update_rows_2, update_rows_3]
    columns = rhs_0.shape[1]
    front_sizes = [PIVOTS >> depth_now for depth_now in range(LEVELS)]
    offsets = [0]
    for depth_now in range(1, LEVELS):
        offsets.append(offsets[-1] + front_sizes[depth_now - 1])
    received = [jnp.zeros((PIVOTS, columns), jnp.float32) for upper in range(LEVELS - 1)]
    forwards = [[None] * (2 ** depth_now) for depth_now in range(LEVELS)]
    for depth_now in reversed(range(LEVELS)):
        front_rows = front_sizes[depth_now]
        for front in range(2 ** depth_now):
            row_start = front * front_rows
            summed = rhs_all[depth_now][row_start:row_start + front_rows].astype(jnp.float32)
            if depth_now < LEVELS - 1:
                summed = summed + received[depth_now][row_start:row_start + front_rows]
            combined = summed.astype(jnp.bfloat16)
            values = jnp.dot(inv_all[depth_now][row_start:row_start + front_rows], combined, preferred_element_type=jnp.float32).astype(jnp.bfloat16)
            forwards[depth_now][front] = values
            if depth_now > 0:
                block = coupling_all[depth_now][row_start:row_start + front_rows]
                update = jnp.dot(block.T, values, preferred_element_type=jnp.float32)
                row_list = lists_all[depth_now][front]
                chain = jnp.zeros((offsets[depth_now], columns), jnp.float32).at[row_list].add(update)
                for upper in range(depth_now):
                    owner = front >> (depth_now - upper)
                    upper_rows = front_sizes[upper]
                    received[upper] = received[upper].at[owner * upper_rows:(owner + 1) * upper_rows].add(chain[offsets[upper]:offsets[upper] + upper_rows])
    solved_all = [[None] * (2 ** depth_now) for depth_now in range(LEVELS)]
    for depth_now in range(LEVELS):
        front_rows = front_sizes[depth_now]
        for front in range(2 ** depth_now):
            row_start = front * front_rows
            values = forwards[depth_now][front]
            if depth_now > 0:
                anc_values = jnp.concatenate([solved_all[upper][front >> (depth_now - upper)] for upper in range(depth_now)], axis=0)
                row_list = lists_all[depth_now][front]
                picked = jnp.take(anc_values, row_list, axis=0)
                block = coupling_all[depth_now][row_start:row_start + front_rows]
                pulled = jnp.dot(block, picked, preferred_element_type=jnp.float32)
                adjusted = (values.astype(jnp.float32) - pulled).astype(jnp.bfloat16)
            else:
                adjusted = values
            inverse = inv_all[depth_now][row_start:row_start + front_rows]
            solved_all[depth_now][front] = jnp.dot(inverse.T, adjusted, preferred_element_type=jnp.float32).astype(jnp.bfloat16)
    outputs = [jnp.concatenate(solved_all[depth_now], axis=0) for depth_now in range(LEVELS)]
    return (outputs[0], outputs[1], outputs[2], outputs[3])
```

```python
import functools

import jax
import jax.numpy as jnp
from jax import lax
from jax.experimental import pallas as pl
from jax.sharding import Mesh
from jax.sharding import PartitionSpec as P

PIVOTS = 4096
LEVELS = 4
BLOCK = 128
HALF = 64
CHUNK = 256
INTERPRET = False

CHIPS = ("ya", "yb", "yc", "x")
GROUP_AXES = (CHIPS, CHIPS[1:], CHIPS[2:], CHIPS[3:])
GROUP_SIZE = (32, 16, 8, 4)
LEAF = ("ya", "yb", "yc", "x", "c")


def exchange(value, axes):
    return lax.all_to_all(value, axes, 0, 0, tiled=True)


def dot_nt(left, right):
    return lax.dot_general(left, right, (((1,), (1,)), ((), ())), preferred_element_type=jnp.float32)


def dot_nn(left, right):
    return lax.dot_general(left, right, (((1,), (0,)), ((), ())), preferred_element_type=jnp.float32)


def call(kernel, out_shapes, inputs):
    specs = []
    arrays = []
    for item in inputs:
        array, shape, index = item if isinstance(item, tuple) else (item, item.shape, (0,) * item.ndim)
        specs.append(pl.BlockSpec(shape, functools.partial(lambda at, _: at, index)))
        arrays.append(array)
    out_specs = [pl.BlockSpec(o.shape, functools.partial(lambda at, _: at, (0,) * len(o.shape))) for o in out_shapes]
    return pl.pallas_call(
        kernel, grid=(1,), in_specs=specs, out_specs=out_specs, out_shape=out_shapes, interpret=INTERPRET
    )(*arrays)


def bf16(*shape):
    return jax.ShapeDtypeStruct(shape, jnp.bfloat16)


def expand_kernel(list_ref, block_ref, out_ref):
    block = block_ref[...]
    rows = list_ref[...]
    width = block.shape[1]
    lane = lax.broadcasted_iota(jnp.int32, (CHUNK, width), 0).astype(jnp.float32).astype(jnp.bfloat16)

    def step(at, carry):
        shifted = jnp.clip(rows - at * CHUNK, -1, CHUNK).astype(jnp.float32).astype(jnp.bfloat16)
        hit = jnp.where(shifted == lane, jnp.bfloat16(1), jnp.bfloat16(0))
        out_ref[pl.ds(pl.multiple_of(at * CHUNK, CHUNK), CHUNK), :] = dot_nt(hit, block).astype(jnp.bfloat16)
        return carry

    lax.fori_loop(0, out_ref.shape[0] // CHUNK, step, 0)


def expanded(row_list, block_item, ancestors):
    return call(expand_kernel, [bf16(ancestors, BLOCK)], [row_list, block_item])[0]


def pairs_product(full_ref, weights, count):
    total = None
    for at in range(0, count, 2):
        left = jnp.concatenate([full_ref[at], full_ref[at + 1]], axis=1)
        part = weights(left, at)
        total = part if total is None else total + part
    return total


def front_values(full_ref, inv_ref, count):
    return pairs_product(
        full_ref, lambda left, at: dot_nt(left, inv_ref[:, at * BLOCK : (at + 2) * BLOCK]), count
    ).astype(jnp.bfloat16)


def forward_kernel(deeper, count, send_count, *refs):
    full_ref, inv_ref = refs[:2]
    old = refs[2 : 2 + deeper]
    couplings = refs[2 + deeper : 3 + 2 * deeper]
    values_ref, send_ref = refs[-2:]
    values = front_values(full_ref, inv_ref, count)
    values_ref[...] = values
    stacked = [r[...] for r in old] + [values]
    for at in range(send_count):
        total = None
        for left, ref in zip(stacked, couplings):
            part = dot_nt(left, ref[at * BLOCK : (at + 1) * BLOCK, :])
            total = part if total is None else total + part
        send_ref[at] = total.astype(jnp.bfloat16)


def spread_kernel(count, has_own, *refs):
    parts_ref = refs[0]
    total = refs[1][...].astype(jnp.float32) if has_own else None
    for at in range(count):
        part = parts_ref[at].astype(jnp.float32)
        total = part if total is None else total + part
    result = total.astype(jnp.bfloat16)
    out_ref = refs[1 + has_own]
    if len(refs) > 2 + has_own:
        refs[-1][...] = result
    if len(out_ref.shape) == 2:
        out_ref[...] = result
    else:
        for at in range(count):
            out_ref[at] = result


def root_kernel(full_ref, inv_ref, send_ref):
    values = front_values(full_ref, inv_ref, GROUP_SIZE[0])
    for at in range(GROUP_SIZE[0]):
        send_ref[at] = dot_nn(values, inv_ref[:, at * BLOCK : (at + 1) * BLOCK]).astype(jnp.bfloat16)


def backward_kernel(depth, *refs):
    solved = refs[:depth]
    values_ref, coupling_ref, inv_ref, send_ref = refs[depth:]
    total = values_ref[...].astype(jnp.float32)
    start = 0
    for upper in range(depth):
        base = start

        def product(left, at):
            return dot_nn(left, coupling_ref[base + at * BLOCK : base + (at + 2) * BLOCK, :])

        total = total - pairs_product(solved[upper], product, GROUP_SIZE[upper])
        start += GROUP_SIZE[upper] * BLOCK
    adjusted = total.astype(jnp.bfloat16)
    for at in range(GROUP_SIZE[depth]):
        send_ref[at] = dot_nn(adjusted, inv_ref[:, at * BLOCK : (at + 1) * BLOCK]).astype(jnp.bfloat16)


def gather_rows(parts):
    shard = jnp.concatenate(parts, axis=1)
    panels = lax.axis_size("z")
    rows = exchange(jnp.broadcast_to(shard[None], (panels,) + shard.shape), "z")
    rows = rows.reshape(panels * shard.shape[0], shard.shape[1])
    both = exchange(jnp.broadcast_to(rows[None], (2,) + rows.shape), "c")
    return both.reshape(BLOCK, shard.shape[1])


def body(
    rhs_0, rhs_1, rhs_2, rhs_3, inv_0, inv_1, inv_2, inv_3, coupling_1, coupling_2, coupling_3, rows_1, rows_2, rows_3
):
    stacked = jnp.concatenate([rhs_0, rhs_1, rhs_2, rhs_3], axis=0).T
    halves = exchange(stacked.reshape(2, HALF, 4 * HALF), "c")
    rhs = [
        jnp.concatenate([halves[0][:, k * HALF : (k + 1) * HALF], halves[1][:, k * HALF : (k + 1) * HALF]], axis=1)
        for k in range(LEVELS)
    ]
    low = gather_rows([inv_1, coupling_1, inv_2, coupling_2, inv_3, coupling_3])
    top = gather_rows([inv_0])
    inv = [
        (top, (BLOCK, 4096), (0, 0)),
        (low, (BLOCK, 2048), (0, 0)),
        (low, (BLOCK, 1024), (0, 4)),
        (low, (BLOCK, 512), (0, 12)),
    ]
    coup = [None, (low, (BLOCK, 2048), (0, 1)), (low, (BLOCK, 1024), (0, 5)), (low, (BLOCK, 512), (0, 13))]
    chip = lax.axis_index(CHIPS)
    exp = [None]
    ancestors = 0
    for k, lists in ((1, rows_1), (2, rows_2), (3, rows_3)):
        ancestors += PIVOTS >> (k - 1)
        mine = lax.dynamic_slice_in_dim(lists, chip // GROUP_SIZE[k], 1, 0)
        exp.append(expanded(mine, coup[k], ancestors))

    def spread(parts, own, count, keep):
        outs = [bf16(count, HALF, BLOCK)] + ([bf16(HALF, BLOCK)] if keep else [])
        kernel = functools.partial(spread_kernel, count, int(own is not None))
        return call(kernel, outs, [parts] + ([own] if own is not None else []))

    values = [None] * LEVELS
    sent = jnp.broadcast_to(rhs[3][None], (4, HALF, BLOCK))
    for k in (3, 2, 1):
        full = exchange(sent, GROUP_AXES[k])
        send_count = GROUP_SIZE[k - 1]
        where = sum(PIVOTS >> j for j in range(k - 1)) // (PIVOTS >> (k - 1))
        order = list(range(3, k, -1))
        blocks = [(exp[j], (PIVOTS >> (k - 1), BLOCK), (where, 0)) for j in order + [k]]
        values[k], parts = call(
            functools.partial(forward_kernel, len(order), GROUP_SIZE[k], send_count),
            [bf16(HALF, BLOCK), bf16(send_count, HALF, BLOCK)],
            [full, inv[k]] + [values[j] for j in order] + blocks,
        )
        parts = exchange(parts, GROUP_AXES[k - 1])
        (sent,) = spread(parts, rhs[k - 1], send_count, False)
    full = exchange(sent, CHIPS)
    parts = call(root_kernel, [bf16(GROUP_SIZE[0], HALF, BLOCK)], [full, inv[0]])[0]
    solved = []
    out = []
    for k in range(LEVELS):
        parts = exchange(parts, GROUP_AXES[k])
        if k == LEVELS - 1:
            kernel = functools.partial(spread_kernel, GROUP_SIZE[k], 0)
            out.append(call(kernel, [bf16(HALF, BLOCK)], [parts])[0])
            break
        sent, own = spread(parts, None, GROUP_SIZE[k], True)
        out.append(own)
        solved.append(exchange(sent, GROUP_AXES[k]))
        parts = call(
            functools.partial(backward_kernel, k + 1),
            [bf16(GROUP_SIZE[k + 1], HALF, BLOCK)],
            solved + [values[k + 1], exp[k + 1], inv[k + 1]],
        )[0]
    halves = jnp.stack(
        [jnp.concatenate([o[:, h * HALF : (h + 1) * HALF] for o in out], axis=1) for h in range(2)], axis=0
    )
    rows = exchange(halves, "c").reshape(2 * HALF, 4 * HALF).T
    return tuple(rows[k * HALF : (k + 1) * HALF] for k in range(LEVELS))


def solution(mesh):
    devices = mesh.devices
    fine = Mesh(devices.reshape(2, 2, 2, 4, 2, devices.size // 64), ("ya", "yb", "yc", "x", "c", "z"))
    wide = P(LEAF, "z")
    rows = P(LEAF + ("z",), None)
    return jax.shard_map(
        body,
        mesh=fine,
        in_specs=(wide,) * 4 + (rows,) * 7 + (P(None, None),) * 3,
        out_specs=(wide,) * 4,
        check_vma=False,
    )
```

```python
import functools

import jax
import jax.numpy as jnp
from jax import lax
from jax.experimental import pallas as pl
from jax.sharding import Mesh
from jax.sharding import PartitionSpec as P

LEVELS = 4
BLOCK = 128
HALF = 64
CHUNK = 256
INTERPRET = False

CHIPS = ("ya", "yb", "yc", "x")
GROUP_AXES = (CHIPS, CHIPS[1:], CHIPS[2:], CHIPS[3:])
GROUP_SIZE = (32, 16, 8, 4)
COLUMN = ("ya", "yb", "yc")
LEAF = ("ya", "yb", "yc", "x", "c")


def exchange(value, axes):
    return lax.all_to_all(value, axes, 0, 0, tiled=True)


def dot_nt(left, right):
    return lax.dot_general(left, right, (((1,), (1,)), ((), ())), preferred_element_type=jnp.float32)


def dot_nn(left, right):
    return lax.dot_general(left, right, (((1,), (0,)), ((), ())), preferred_element_type=jnp.float32)


def call(kernel, out_shapes, inputs):
    specs = []
    arrays = []
    for item in inputs:
        array, shape, index = item if isinstance(item, tuple) else (item, item.shape, (0,) * item.ndim)
        specs.append(pl.BlockSpec(shape, functools.partial(lambda at, _: at, index)))
        arrays.append(array)
    out_specs = [pl.BlockSpec(o.shape, functools.partial(lambda at, _: at, (0,) * len(o.shape))) for o in out_shapes]
    return pl.pallas_call(
        kernel, grid=(1,), in_specs=specs, out_specs=out_specs, out_shape=out_shapes, interpret=INTERPRET
    )(*arrays)


def bf16(*shape):
    return jax.ShapeDtypeStruct(shape, jnp.bfloat16)


def expand_kernel(base, list_ref, first_ref, second_ref, out_ref):
    block = jnp.concatenate([first_ref[...], second_ref[...]], axis=0)
    rows = list_ref[...] - base
    width = block.shape[1]
    lane = lax.broadcasted_iota(jnp.int32, (CHUNK, width), 0).astype(jnp.float32).astype(jnp.bfloat16)

    def step(at, carry):
        shifted = jnp.clip(rows - at * CHUNK, -1, CHUNK).astype(jnp.float32).astype(jnp.bfloat16)
        hit = jnp.where(shifted == lane, jnp.bfloat16(1), jnp.bfloat16(0))
        out_ref[pl.ds(pl.multiple_of(at * CHUNK, CHUNK), CHUNK), :] = dot_nt(hit, block).astype(jnp.bfloat16)
        return carry

    lax.fori_loop(0, out_ref.shape[0] // CHUNK, step, 0, unroll=4)


def expanded(row_list, pieces, base, count):
    kernel = functools.partial(expand_kernel, base)
    return call(kernel, [bf16(count, BLOCK)], [row_list] + pieces)[0]


def pairs_product(full_ref, weights, count):
    total = None
    for at in range(0, count, 2):
        left = jnp.concatenate([full_ref[at], full_ref[at + 1]], axis=1)
        part = weights(left, at)
        total = part if total is None else total + part
    return total


def front_values(full_ref, inverse, count, first=0):
    return pairs_product(
        full_ref, lambda left, at: dot_nt(left, inverse[:, first + at * BLOCK : first + (at + 2) * BLOCK]), count
    )


def forward_kernel(deeper, count, send_count, *refs):
    full_ref, first_ref, second_ref = refs[:3]
    old = refs[3 : 3 + deeper]
    couplings = refs[3 + deeper : 4 + 2 * deeper]
    values_ref, send_ref = refs[-2:]
    inverse = jnp.concatenate([first_ref[...], second_ref[...]], axis=0)
    values = front_values(full_ref, inverse, count).astype(jnp.bfloat16)
    values_ref[...] = values
    stacked = [r[...] for r in old] + [values]
    for at in range(send_count):
        total = None
        for left, ref in zip(stacked, couplings):
            part = dot_nt(left, ref[at * BLOCK : (at + 1) * BLOCK, :])
            total = part if total is None else total + part
        send_ref[at] = total.astype(jnp.bfloat16)


def spread_kernel(count, has_own, *refs):
    parts_ref = refs[0]
    total = refs[1][...].astype(jnp.float32) if has_own else None
    for at in range(count):
        part = parts_ref[at].astype(jnp.float32)
        total = part if total is None else total + part
    result = total.astype(jnp.bfloat16)
    for out_ref in refs[1 + has_own :]:
        if len(out_ref.shape) == 2:
            out_ref[...] = result
        else:
            for at in range(out_ref.shape[0]):
                out_ref[at] = result


def root_values_kernel(full_ref, first_ref, second_ref, send_ref):
    inverse = jnp.concatenate([first_ref[...], second_ref[...]], axis=0)
    for part in range(4):
        partial = front_values(full_ref, inverse, 8, part * 8 * BLOCK).astype(jnp.bfloat16)
        for at in range(4):
            send_ref[at, :, part * BLOCK : (part + 1) * BLOCK] = partial


def root_solve_kernel(parts_ref, first_ref, second_ref, send_ref):
    inverse = jnp.concatenate([first_ref[...], second_ref[...]], axis=0)
    total = parts_ref[0].astype(jnp.float32)
    for at in range(1, 4):
        total = total + parts_ref[at].astype(jnp.float32)
    values = total.astype(jnp.bfloat16)
    for at in range(8):
        solved = None
        for part in range(4):
            start = (part * 8 + at) * BLOCK
            piece = dot_nn(values[:, part * BLOCK : (part + 1) * BLOCK], inverse[:, start : start + BLOCK])
            solved = piece if solved is None else solved + piece
        send_ref[at] = solved.astype(jnp.bfloat16)


def backward_kernel(depth, *refs):
    solved = refs[:depth]
    values_ref, first_ref, second_ref = refs[depth : depth + 3]
    couplings = refs[depth + 3 : 2 * depth + 3]
    send_ref = refs[-1]
    total = values_ref[...].astype(jnp.float32)
    for upper in range(depth):

        def product(left, at):
            return dot_nn(left, couplings[upper][at * BLOCK : (at + 2) * BLOCK, :])

        total = total - pairs_product(solved[upper], product, GROUP_SIZE[upper])
    adjusted = total.astype(jnp.bfloat16)
    inverse = jnp.concatenate([first_ref[...], second_ref[...]], axis=0)
    for at in range(GROUP_SIZE[depth]):
        send_ref[at] = dot_nn(adjusted, inverse[:, at * BLOCK : (at + 1) * BLOCK]).astype(jnp.bfloat16)


def copies_kernel(*refs):
    out_ref = refs[-1]
    for at in range(out_ref.shape[0]):
        start = 0
        for ref in refs[:-1]:
            width = ref.shape[1]
            out_ref[at, :, start : start + width] = ref[...]
            start += width


def partner(value, axis, mask):
    size = lax.axis_size(axis)
    return lax.ppermute(value, axis, [(at, at ^ mask) for at in range(size)])


def in_order(mine, other, axis):
    low = lax.axis_index("c") == 0
    first = jnp.where(low, mine, other)
    second = jnp.where(low, other, mine)
    return jnp.concatenate([first, second], axis=axis)


def solve(
    rhs_0, rhs_1, rhs_2, rhs_3, inv_0, inv_1, inv_2, inv_3, coupling_1, coupling_2, coupling_3, rows_1, rows_2, rows_3
):
    panels = lax.axis_size("z")
    shard_rows = inv_0.shape[0]
    core = lax.axis_index("c")
    copies = call(copies_kernel, [bf16(panels, shard_rows, 3072)], [inv_2, coupling_2, inv_3, coupling_3])[0]
    low = exchange(copies, "z").reshape(HALF, 3072)
    stacked = jnp.concatenate([rhs_0, rhs_1, rhs_2, rhs_3], axis=0).T
    mine = lax.dynamic_slice_in_dim(stacked, core * HALF, HALF, 0)
    other = partner(lax.dynamic_slice_in_dim(stacked, (1 - core) * HALF, HALF, 0), "c", 1)
    rhs = [in_order(mine[:, k * HALF : (k + 1) * HALF], other[:, k * HALF : (k + 1) * HALF], 1) for k in range(LEVELS)]
    low = [low, partner(low, "c", 1)]
    top = inv_0.reshape(shard_rows, 8, 4, BLOCK).transpose(2, 1, 0, 3).reshape(4, 8 * shard_rows, BLOCK)
    sent = jnp.concatenate([jnp.broadcast_to(rhs[3][None], (4, HALF, BLOCK)), top], axis=1)
    full = exchange(sent, "x")
    top = full[:, HALF:].reshape(32, shard_rows, BLOCK).transpose(1, 0, 2).reshape(shard_rows, 4096)
    high = jnp.concatenate([inv_1, coupling_1, top], axis=1)
    mask = panels // 2
    while mask:
        high = jnp.concatenate([high, partner(high, "z", mask)], axis=0)
        mask //= 2
    high = [high, partner(high, "c", 1)]

    def pieces(arrays, width, at):
        return [(a, (HALF, width), (0, at)) for a in arrays]

    inv = [pieces(high, 4096, 1), pieces(high, 2048, 0), pieces(low, 1024, 0), pieces(low, 512, 4)]
    coup = [None, pieces(high, 2048, 1), pieces(low, 1024, 1), pieces(low, 512, 5)]
    chip = lax.axis_index(CHIPS)
    lists = [None] + [
        lax.dynamic_slice_in_dim(rows, chip // GROUP_SIZE[k], 1, 0)
        for k, rows in ((1, rows_1), (2, rows_2), (3, rows_3))
    ]
    near_3 = expanded(lists[3], coup[3], 6144, 1024)
    near_2 = expanded(lists[2], coup[2], 4096, 2048)
    far_3 = expanded(lists[3], coup[3], 0, 6144)
    far_2 = expanded(lists[2], coup[2], 0, 4096)
    near_1 = expanded(lists[1], coup[1], 0, 4096)
    to_0 = lambda a: (a, (4096, BLOCK), (0, 0))
    far_31 = (far_3, (2048, BLOCK), (2, 0))
    exp = [None, [near_1], [to_0(far_2), near_2], [to_0(far_3), far_31, near_3]]

    values = [None] * LEVELS
    full = (full, (4, HALF, BLOCK), (0, 0, 0))
    for k in (3, 2, 1):
        send_count = GROUP_SIZE[k - 1]
        order = list(range(3, k, -1))
        values[k], parts = call(
            functools.partial(forward_kernel, len(order), GROUP_SIZE[k], send_count),
            [bf16(HALF, BLOCK), bf16(send_count, HALF, BLOCK)],
            [full] + inv[k] + [values[j] for j in order] + [exp[j][k - 1] for j in order + [k]],
        )
        parts = exchange(parts, GROUP_AXES[k - 1])
        spread_count = send_count if k > 1 else 8
        sent = call(
            functools.partial(spread_kernel, send_count, 1), [bf16(spread_count, HALF, BLOCK)], [parts, rhs[k - 1]]
        )[0]
        full = exchange(sent, GROUP_AXES[k - 1] if k > 1 else COLUMN)
    parts = call(root_values_kernel, [bf16(4, HALF, 4 * BLOCK)], [full] + inv[0])[0]
    parts = exchange(parts, "x")
    parts = call(root_solve_kernel, [bf16(8, HALF, BLOCK)], [parts] + inv[0])[0]
    solved = []
    out = []
    for k in range(LEVELS):
        parts = exchange(parts, GROUP_AXES[k] if k else COLUMN)
        kernel = functools.partial(spread_kernel, GROUP_SIZE[k] if k else 8, 0)
        if k == LEVELS - 1:
            out.append(call(kernel, [bf16(HALF, BLOCK)], [parts])[0])
            break
        sent, own = call(kernel, [bf16(GROUP_SIZE[k], HALF, BLOCK), bf16(HALF, BLOCK)], [parts])
        out.append(own)
        solved.append(exchange(sent, GROUP_AXES[k]))
        parts = call(
            functools.partial(backward_kernel, k + 1),
            [bf16(GROUP_SIZE[k + 1], HALF, BLOCK)],
            solved + [values[k + 1]] + inv[k + 1] + exp[k + 1],
        )[0]
    lows = jnp.concatenate([o[:, :HALF] for o in out], axis=1)
    highs = jnp.concatenate([o[:, HALF:] for o in out], axis=1)
    low_core = core == 0
    other = partner(jnp.where(low_core, highs, lows), "c", 1)
    rows = in_order(jnp.where(low_core, lows, highs), other, 0).T
    return tuple(rows[k * HALF : (k + 1) * HALF] for k in range(LEVELS))


def solution(mesh):
    devices = mesh.devices
    fine = Mesh(devices.reshape(2, 2, 2, 4, 2, devices.size // 64), ("ya", "yb", "yc", "x", "c", "z"))
    wide = P(LEAF, "z")
    rows = P(LEAF + ("z",), None)
    return jax.shard_map(
        solve,
        mesh=fine,
        in_specs=(wide,) * 4 + (rows,) * 7 + (P(None, None),) * 3,
        out_specs=(wide,) * 4,
        check_vma=False,
    )
```

```python
import functools

import jax
import jax.numpy as jnp
from jax import lax
from jax.experimental import pallas as pl
from jax.sharding import Mesh
from jax.sharding import PartitionSpec as P

LEVELS = 4
BLOCK = 128
HALF = 64
CHUNK = 256
WIDE = 4
INTERPRET = False

CHIPS = ("ya", "yb", "yc", "x")
GROUP_AXES = (CHIPS, CHIPS[1:], CHIPS[2:], CHIPS[3:])
GROUP_SIZE = (32, 16, 8, 4)
COLUMN = ("ya", "yb", "yc")
LEAF = ("ya", "yb", "yc", "x", "c")


def exchange(value, axes):
    return lax.all_to_all(value, axes, 0, 0, tiled=True)


def dot_nt(left, right):
    return lax.dot_general(left, right, (((1,), (1,)), ((), ())), preferred_element_type=jnp.float32)


def dot_nn(left, right):
    return lax.dot_general(left, right, (((1,), (0,)), ((), ())), preferred_element_type=jnp.float32)


def call(kernel, out_shapes, inputs):
    specs = []
    arrays = []
    for item in inputs:
        array, shape, index = item if isinstance(item, tuple) else (item, item.shape, (0,) * item.ndim)
        specs.append(pl.BlockSpec(shape, functools.partial(lambda at, _: at, index)))
        arrays.append(array)
    out_specs = [pl.BlockSpec(o.shape, functools.partial(lambda at, _: at, (0,) * len(o.shape))) for o in out_shapes]
    return pl.pallas_call(
        kernel, grid=(1,), in_specs=specs, out_specs=out_specs, out_shape=out_shapes, interpret=INTERPRET
    )(*arrays)


def bf16(*shape):
    return jax.ShapeDtypeStruct(shape, jnp.bfloat16)


def expand_kernel(base, list_ref, first_ref, second_ref, out_ref):
    block = jnp.concatenate([first_ref[...], second_ref[...]], axis=0)
    rows = list_ref[...] - base
    width = block.shape[1]
    lane = lax.broadcasted_iota(jnp.int32, (CHUNK, width), 0).astype(jnp.float32).astype(jnp.bfloat16)

    def step(at, carry):
        shifted = jnp.clip(rows - at * CHUNK, -1, CHUNK).astype(jnp.float32).astype(jnp.bfloat16)
        hit = jnp.where(shifted == lane, jnp.bfloat16(1), jnp.bfloat16(0))
        out_ref[pl.ds(pl.multiple_of(at * CHUNK, CHUNK), CHUNK), :] = dot_nt(hit, block).astype(jnp.bfloat16)
        return carry

    lax.fori_loop(0, out_ref.shape[0] // CHUNK, step, 0, unroll=4)


def expanded(row_list, pieces, base, count):
    kernel = functools.partial(expand_kernel, base)
    return call(kernel, [bf16(count, BLOCK)], [row_list] + pieces)[0]


def pairs_product(full_ref, weights, count):
    total = None
    for at in range(0, count, 2):
        left = jnp.concatenate([full_ref[at], full_ref[at + 1]], axis=1)
        part = weights(left, at)
        total = part if total is None else total + part
    return total


def front_values(full_ref, inverse, count, first=0):
    return pairs_product(
        full_ref, lambda left, at: dot_nt(left, inverse[:, first + at * BLOCK : first + (at + 2) * BLOCK]), count
    )


def put_blocks(send_ref, at, total):
    for step in range(WIDE):
        send_ref[at + step] = total[:, step * BLOCK : (step + 1) * BLOCK].astype(jnp.bfloat16)


def forward_kernel(deeper, count, send_count, *refs):
    full_ref, first_ref, second_ref = refs[:3]
    old = refs[3 : 3 + deeper]
    couplings = refs[3 + deeper : 4 + 2 * deeper]
    values_ref, send_ref = refs[-2:]
    inverse = jnp.concatenate([first_ref[...], second_ref[...]], axis=0)
    values = front_values(full_ref, inverse, count).astype(jnp.bfloat16)
    values_ref[...] = values
    stacked = [r[...] for r in old] + [values]
    for at in range(0, send_count, WIDE):
        total = None
        for left, ref in zip(stacked, couplings):
            part = dot_nt(left, ref[at * BLOCK : (at + WIDE) * BLOCK, :])
            total = part if total is None else total + part
        put_blocks(send_ref, at, total)


def spread_kernel(count, has_own, *refs):
    parts_ref = refs[0]
    total = refs[1][...].astype(jnp.float32) if has_own else None
    for at in range(count):
        part = parts_ref[at].astype(jnp.float32)
        total = part if total is None else total + part
    result = total.astype(jnp.bfloat16)
    for out_ref in refs[1 + has_own :]:
        if len(out_ref.shape) == 2:
            out_ref[...] = result
        else:
            for at in range(out_ref.shape[0]):
                out_ref[at] = result


def root_values_kernel(full_ref, first_ref, second_ref, send_ref):
    inverse = jnp.concatenate([first_ref[...], second_ref[...]], axis=0)
    for part in range(4):
        partial = front_values(full_ref, inverse, 8, part * 8 * BLOCK).astype(jnp.bfloat16)
        for at in range(4):
            send_ref[at, :, part * BLOCK : (part + 1) * BLOCK] = partial


def root_solve_kernel(parts_ref, first_ref, second_ref, send_ref):
    inverse = jnp.concatenate([first_ref[...], second_ref[...]], axis=0)
    total = parts_ref[0].astype(jnp.float32)
    for at in range(1, 4):
        total = total + parts_ref[at].astype(jnp.float32)
    values = total.astype(jnp.bfloat16)
    for at in range(0, 8, WIDE):
        solved = None
        for part in range(4):
            start = (part * 8 + at) * BLOCK
            piece = dot_nn(values[:, part * BLOCK : (part + 1) * BLOCK], inverse[:, start : start + WIDE * BLOCK])
            solved = piece if solved is None else solved + piece
        put_blocks(send_ref, at, solved)


def pulled(total, solved, couplings, first):
    for upper, (full_ref, coupling_ref) in enumerate(zip(solved, couplings), first):

        def product(left, at):
            return dot_nn(left, coupling_ref[at * BLOCK : (at + 2) * BLOCK, :])

        total = total - pairs_product(full_ref, product, GROUP_SIZE[upper])
    return total


def top_pull_kernel(full_ref, *refs):
    count = len(refs) // 3
    for at in range(count):
        total = refs[at][...].astype(jnp.float32)
        refs[2 * count + at][...] = pulled(total, [full_ref], [refs[count + at]], 0)


def backward_kernel(depth, first, *refs):
    count = depth - first
    values_ref, first_ref, second_ref = refs[count : count + 3]
    send_ref = refs[-1]
    total = values_ref[...].astype(jnp.float32)
    adjusted = pulled(total, refs[:count], refs[count + 3 : -1], first).astype(jnp.bfloat16)
    inverse = jnp.concatenate([first_ref[...], second_ref[...]], axis=0)
    if depth == LEVELS - 1:
        solved = dot_nn(adjusted, inverse)
        for at in range(2 * GROUP_SIZE[depth]):
            block = solved[:, at * HALF : (at + 1) * HALF]
            send_ref[at] = jnp.concatenate([block[: HALF // 2], block[HALF // 2 :]], axis=1).astype(jnp.bfloat16)
        return
    for at in range(0, GROUP_SIZE[depth], WIDE):
        put_blocks(send_ref, at, dot_nn(adjusted, inverse[:, at * BLOCK : (at + WIDE) * BLOCK]))


def final_kernel(parts_ref, out_ref):
    halves = []
    for core in range(2):
        total = parts_ref[core].astype(jnp.float32)
        for at in range(1, GROUP_SIZE[-1]):
            total = total + parts_ref[2 * at + core].astype(jnp.float32)
        halves += [total[:, :HALF], total[:, HALF:]]
    out_ref[...] = jnp.concatenate(halves, axis=0).T.astype(jnp.bfloat16)


def copies_kernel(*refs):
    out_ref = refs[-1]
    for at in range(out_ref.shape[0]):
        start = 0
        for ref in refs[:-1]:
            width = ref.shape[1]
            out_ref[at, :, start : start + width] = ref[...]
            start += width


def partner(value, axis, mask):
    size = lax.axis_size(axis)
    return lax.ppermute(value, axis, [(at, at ^ mask) for at in range(size)])


def by_chip(blocks):
    chip = lax.axis_index("x")
    odd = (chip & 1) == 1
    high = (chip & 2) == 2
    pairs = []
    for at in (0, 2):
        pairs += [jnp.where(odd, blocks[at + 1], blocks[at]), jnp.where(odd, blocks[at], blocks[at + 1])]
    return [jnp.where(high, pairs[at ^ 2], pairs[at]) for at in range(4)]


def in_order(mine, other, axis):
    low = lax.axis_index("c") == 0
    first = jnp.where(low, mine, other)
    second = jnp.where(low, other, mine)
    return jnp.concatenate([first, second], axis=axis)


def solve(
    rhs_0, rhs_1, rhs_2, rhs_3, inv_0, inv_1, inv_2, inv_3, coupling_1, coupling_2, coupling_3, rows_1, rows_2, rows_3
):
    panels = lax.axis_size("z")
    shard_rows = inv_0.shape[0]
    core = lax.axis_index("c")
    copies = call(copies_kernel, [bf16(panels, shard_rows, 3072)], [inv_2, coupling_2, inv_3, coupling_3])[0]
    low = exchange(copies, "z").reshape(HALF, 3072)
    stacked = jnp.concatenate([rhs_0, rhs_1, rhs_2, rhs_3], axis=0).T
    mine = lax.dynamic_slice_in_dim(stacked, core * HALF, HALF, 0)
    other = partner(lax.dynamic_slice_in_dim(stacked, (1 - core) * HALF, HALF, 0), "c", 1)
    rhs = [in_order(mine[:, k * HALF : (k + 1) * HALF], other[:, k * HALF : (k + 1) * HALF], 1) for k in range(LEVELS)]
    low = [low, partner(low, "c", 1)]
    full = jnp.stack(by_chip([rhs[3]] + [partner(rhs[3], "x", mask) for mask in (1, 2, 3)]))
    top = inv_0.reshape(shard_rows, 8, 4, BLOCK).transpose(2, 0, 1, 3).reshape(4, shard_rows, 8 * BLOCK)
    spot = lax.axis_index("x")
    tops = [lax.dynamic_index_in_dim(top, spot ^ mask, 0, keepdims=False) for mask in range(4)]
    top = by_chip(tops[:1] + [partner(tops[mask], "x", mask) for mask in (1, 2, 3)])
    top = jnp.concatenate(top, axis=1)
    high = jnp.concatenate([inv_1, coupling_1, top], axis=1)
    mask = panels // 2
    while mask:
        high = jnp.concatenate([high, partner(high, "z", mask)], axis=0)
        mask //= 2
    high = [high, partner(high, "c", 1)]

    def pieces(arrays, width, at):
        return [(a, (HALF, width), (0, at)) for a in arrays]

    inv = [pieces(high, 4096, 1), pieces(high, 2048, 0), pieces(low, 1024, 0), pieces(low, 512, 4)]
    coup = [None, pieces(high, 2048, 1), pieces(low, 1024, 1), pieces(low, 512, 5)]
    chip = lax.axis_index(CHIPS)
    lists = [None] + [
        lax.dynamic_slice_in_dim(rows, chip // GROUP_SIZE[k], 1, 0)
        for k, rows in ((1, rows_1), (2, rows_2), (3, rows_3))
    ]
    near_3 = expanded(lists[3], coup[3], 6144, 1024)
    near_2 = expanded(lists[2], coup[2], 4096, 2048)
    far_3 = expanded(lists[3], coup[3], 0, 6144)
    far_2 = expanded(lists[2], coup[2], 0, 4096)
    near_1 = expanded(lists[1], coup[1], 0, 4096)
    to_0 = lambda a: (a, (4096, BLOCK), (0, 0))
    far_31 = (far_3, (2048, BLOCK), (2, 0))
    exp = [None, [near_1], [to_0(far_2), near_2], [to_0(far_3), far_31, near_3]]

    values = [None] * LEVELS
    for k in (3, 2, 1):
        send_count = GROUP_SIZE[k - 1]
        order = list(range(3, k, -1))
        values[k], parts = call(
            functools.partial(forward_kernel, len(order), GROUP_SIZE[k], send_count),
            [bf16(HALF, BLOCK), bf16(send_count, HALF, BLOCK)],
            [full] + inv[k] + [values[j] for j in order] + [exp[j][k - 1] for j in order + [k]],
        )
        parts = exchange(parts, GROUP_AXES[k - 1])
        spread_count = send_count if k > 1 else 8
        sent = call(
            functools.partial(spread_kernel, send_count, 1), [bf16(spread_count, HALF, BLOCK)], [parts, rhs[k - 1]]
        )[0]
        full = exchange(sent, GROUP_AXES[k - 1] if k > 1 else COLUMN)
    parts = call(root_values_kernel, [bf16(4, HALF, 4 * BLOCK)], [full] + inv[0])[0]
    parts = exchange(parts, "x")
    parts = call(root_solve_kernel, [bf16(8, HALF, BLOCK)], [parts] + inv[0])[0]
    solved = []
    out = []
    for k in range(LEVELS - 1):
        parts = exchange(parts, GROUP_AXES[k] if k else COLUMN)
        kernel = functools.partial(spread_kernel, GROUP_SIZE[k] if k else 8, 0)
        sent, own = call(kernel, [bf16(GROUP_SIZE[k], HALF, BLOCK), bf16(HALF, BLOCK)], [parts])
        out.append(own)
        solved.append(exchange(sent, GROUP_AXES[k]))
        if k == 1:
            values[2:] = call(
                top_pull_kernel,
                [jax.ShapeDtypeStruct((HALF, BLOCK), jnp.float32)] * 2,
                [solved[0]] + values[2:] + [exp[2][0], exp[3][0]],
            )
        first = 1 if k else 0
        send_shape = bf16(GROUP_SIZE[k + 1], HALF, BLOCK) if k < LEVELS - 2 else bf16(8, HALF // 2, BLOCK)
        parts = call(
            functools.partial(backward_kernel, k + 1, first),
            [send_shape],
            solved[first:] + [values[k + 1]] + inv[k + 1] + exp[k + 1][first:],
        )[0]
    outputs = returned(out[:2], core) + returned(out[2:], core)
    parts = exchange(parts, ("x", "c"))
    outputs += call(final_kernel, [bf16(HALF, BLOCK)], [parts])
    return tuple(outputs)


def returned(solved, core):
    lows = jnp.concatenate([o[:, :HALF] for o in solved], axis=1)
    highs = jnp.concatenate([o[:, HALF:] for o in solved], axis=1)
    low_core = core == 0
    other = partner(jnp.where(low_core, highs, lows), "c", 1)
    rows = in_order(jnp.where(low_core, lows, highs), other, 0).T
    return [rows[k * HALF : (k + 1) * HALF] for k in range(len(solved))]


def solution(mesh):
    devices = mesh.devices
    fine = Mesh(devices.reshape(2, 2, 2, 4, 2, devices.size // 64), ("ya", "yb", "yc", "x", "c", "z"))
    wide = P(LEAF, "z")
    rows = P(LEAF + ("z",), None)
    return jax.shard_map(
        solve,
        mesh=fine,
        in_specs=(wide,) * 4 + (rows,) * 7 + (P(None, None),) * 3,
        out_specs=(wide,) * 4,
        check_vma=False,
    )
```
